32 devices in a mesh: real: 2 (over x), tile: 16 (over z, y, core).
Axes of the slice: x: 2, y: 2, z: 4, core: 2. Of those that a mesh axis runs over, the one named last changes fastest.
Arguments:
- positions: float32 [6, 8192], P('real', 'tile'), parts along dimension 0, may hold values from -1.5 to 125.5, as said below
- residual: float32 [6, 8192], P('real', 'tile'), parts along dimension 0, may hold values from -24 to 24
- iterate: float32 [6, 8192], P('real', 'tile'), parts along dimension 0, may hold values from -6 to 6
Outputs:
- new_iterate: float32 [6, 8192], P('real', 'tile'), parts along dimension 0
- new_residual: float32 [6, 8192], P('real', 'tile'), parts along dimension 0
- new_direction: float32 [6, 8192], P('real', 'tile'), parts along dimension 0
The draws below stay inside these ranges and needn't reach their ends.
There are 2 independent parts, one for each index of `real`. The reference program is written for one: setup_inputs(seed, part) draws one part's arguments, and reference() takes and returns one part's arrays. A program takes and returns all parts, laid end to end along the dimension named above; each array names one. Nothing has to cross between parts.
Inputs may be any that keep to these rules, and one draw needn't show every extreme that they name: `positions`: distinct blobs are at least 1 apart.
All inputs are finite; a program needn't handle non-finite values.
Results may differ from the reference program's by a relative error of at most 0.0003.
Values sent between devices are 32-bit elements; how exact they have to be, the bound alone decides.
A program may use at most 64 MiB of HBM per device.

```python
import math
import jax
import jax.numpy as jnp
from jax import lax

BLOB_DEV = 512
BLOBS = 8192


def lattice_coords(key):
    lattice_site = jax.random.permutation(jax.random.fold_in(key, 5), BLOBS).astype(jnp.int32)
    return jnp.stack([lattice_site % 32, lattice_site // 32 % 32, lattice_site // 1024]).astype(jnp.float32) * 4.0


def smooth_flow(key, strength):
    coords = lattice_coords(key) + 2.0
    layers = (BLOBS + 1023) // 1024
    extent = jnp.array([128.0, 128.0, 4.0 * layers], jnp.float32)[:, None]
    modes = jax.random.randint(jax.random.fold_in(key, 31), (3,), 1, 3).astype(jnp.float32)[:, None]
    flip = jax.random.randint(jax.random.fold_in(key, 32), (), 0, 2).astype(jnp.float32) * 2.0 - 1.0
    rate = math.pi * modes / extent
    phase = rate * coords
    sines = jnp.sin(phase)
    cosines = jnp.cos(phase)
    first = rate[0] * cosines[0] * sines[1] * sines[2]
    second = rate[1] * sines[0] * cosines[1] * sines[2]
    third = rate[2] * sines[0] * sines[1] * cosines[2]
    length = jnp.sqrt(jnp.sum(rate * rate))
    return flip * strength * jnp.stack([first, second, third]) / length


def draw_positions(key, part):
    lattice = lattice_coords(key)
    jitter = jnp.clip(0.6 * jax.random.normal(jax.random.fold_in(key, 11), (3, BLOBS), jnp.float32), -1.5, 1.5)
    return lattice + jitter


def draw_residual(key, part):
    number = jnp.arange(BLOBS, dtype=jnp.int32).astype(jnp.float32)
    growth = 1.0 + 2.0 * number / (BLOBS - 1)
    normal_part = jnp.clip(jax.random.normal(jax.random.fold_in(key, 21), (3, BLOBS), jnp.float32), -3.3, 3.3)
    row_scale = jnp.exp(jax.random.uniform(jax.random.fold_in(key, 22), (3, BLOBS), jnp.float32, 0.0, math.log(10.0)))
    return 0.2 * normal_part * row_scale * growth[None, :] + smooth_flow(key, 2.0)


def steps_of(stream_key, shape, cuts, low, high):
    factor_of, own = 1.0, jax.random.fold_in(stream_key, 6)
    for position, parts in cuts:
        draws = jnp.exp(jax.random.uniform(jax.random.fold_in(own, position), (parts,), jnp.float32, low / len(cuts), high / len(cuts)))
        factor_of = factor_of * jnp.repeat(draws, shape[position] // parts).reshape([-1 if axis == position else 1 for axis in range(len(shape))])
    return factor_of


def bell_draw(rng, shape, width, bound, split=(), held_as=jnp.bfloat16):
    entries = width * jax.random.normal(rng, shape, jnp.float32)
    if split:
        entries = entries * steps_of(rng, shape, split, -0.22, 0.18)
    return jnp.clip(entries, -bound, bound).astype(held_as)


def setup_inputs(seed: int = 0, part: int = 0) -> dict:
    keys = jax.random.split(jax.random.key(seed), 4)
    own_keys = jax.random.split(jax.random.fold_in(keys[3], part), 4)
    positions = draw_positions(jax.random.fold_in(jax.random.fold_in(keys[3], part), 71), part)
    residual = draw_residual(jax.random.fold_in(jax.random.fold_in(keys[3], part), 71), part)
    iterate = bell_draw(own_keys[2], (3, BLOBS), 1.0, 6.0, ((1, 16),), jnp.float32)
    return dict(positions=positions, residual=residual, iterate=iterate)


def pair_terms(row_pos, col_pos):
    separation = row_pos[:, :, None] - col_pos[:, None, :]
    squared = lax.optimization_barrier(jnp.sum(separation * separation, axis=0))
    radius = jnp.sqrt(squared)
    inverse = 1.0 / jnp.maximum(radius, 0.5)
    inverse_sq = inverse * inverse
    far_scalar = 0.75 * inverse * (1.0 + 2.0 / 3.0 * inverse_sq)
    far_tensor = 0.75 * (1.0 - 2.0 * inverse_sq) * inverse_sq * inverse
    touching = radius < 2.0
    scalar_part = jnp.where(touching, 1.0 - 9.0 / 32.0 * radius, far_scalar)
    tensor_part = jnp.where(touching, 3.0 / 32.0 * inverse, far_tensor)
    return (separation, scalar_part, tensor_part)

def toward_rows(separation, scalar_part, tensor_part, col_forces):
    projected = lax.optimization_barrier(jnp.sum(separation * col_forces[:, None, :], axis=0))
    return lax.optimization_barrier(jnp.sum(scalar_part[None] * col_forces[:, None, :] + (tensor_part * projected)[None] * separation, axis=2))

def reference(positions, residual, iterate):
    row_block = 256 if BLOBS % 256 == 0 else BLOB_DEV
    block_count = BLOBS // row_block
    stacked = positions.reshape(3, block_count, row_block).transpose(1, 0, 2)

    def block_image(row_pos):
        separation, scalar_part, tensor_part = pair_terms(row_pos, positions)
        return toward_rows(separation, scalar_part, tensor_part, residual)
    applied = lax.map(block_image, stacked).transpose(1, 0, 2).reshape(3, BLOBS)
    old_norm = jnp.sum(residual * residual)
    curvature = jnp.sum(residual * applied)
    step_size = old_norm / curvature
    new_iterate = iterate + step_size * residual
    new_residual = residual - step_size * applied
    new_norm = jnp.sum(new_residual * new_residual)
    new_direction = new_residual + new_norm / old_norm * residual
    return (new_iterate, new_residual, new_direction)
```

```python
import functools
import math

import jax
import jax.numpy as jnp
from jax import lax
from jax.experimental import pallas as pl
from jax.experimental.pallas import tpu as pltpu
from jax.sharding import PartitionSpec as P

MESH = pl.DeviceIdType.MESH
CENTRE = 62.0
SCALE = math.sqrt(0.75)
TOUCH = math.sqrt(3.0)
FACTOR = SCALE**3 / 2.0
ROWS = 128
KDIM = 64


def split3(x):
    high = x.astype(jnp.bfloat16).astype(jnp.float32)
    rest = x - high
    mid = rest.astype(jnp.bfloat16).astype(jnp.float32)
    return high, mid, rest - mid


def split2(x):
    high = x.astype(jnp.bfloat16)
    return high, (x - high.astype(jnp.float32)).astype(jnp.bfloat16)


def dot_nn(a, b):
    return lax.dot_general(a, b, (((1,), (0,)), ((), ())), preferred_element_type=jnp.float32)


def dot_nt(a, b):
    return lax.dot_general(a, b, (((1,), (1,)), ((), ())), preferred_element_type=jnp.float32)


def features(x):
    high, mid, low = split3(x)
    row = lax.broadcasted_iota(jnp.int32, x.shape, 0)
    ones = jnp.where(row < 3, 1.0, 0.0).astype(jnp.float32)
    return jnp.concatenate(
        [high, mid, low, high, mid, high, ones, jnp.zeros_like(x)], axis=0
    ).astype(jnp.bfloat16)


def own_features(x):
    high, mid, low = split3(x)
    row = lax.broadcasted_iota(jnp.int32, x.shape, 0)
    zero = jnp.zeros_like(x)
    is_pos = row < 3
    near = [jnp.where(is_pos, -2.0 * part, zero) for part in (high, mid, low)]
    near[0] = jnp.where(row == 3, 1.0, near[0])
    shifted = [jnp.where((row >= 4) & (row < 7), pltpu.roll(part, 4, 0), zero) for part in (high, mid, low)]
    shifted[0] = jnp.where(row == 7, -1.0, shifted[0])
    own = jnp.where(row == 0, high[3:4], jnp.where(row == 1, mid[3:4], jnp.where(row == 2, low[3:4], zero)))

    def stack(parts, last):
        h, m, l = parts
        return jnp.concatenate([h, h, h, m, m, l, last, zero], axis=0)

    both = jnp.concatenate([stack(near, own), stack(shifted, zero)], axis=0)
    return both.T


def pair_block(cols, own_ref, acc_f, acc_g, diagonal):
    size = own_ref.shape[1]
    for start in range(0, size, ROWS):
        rows = slice(start, start + ROWS)
        squared = dot_nn(own_ref[0, rows, :], cols)
        projected = dot_nn(own_ref[1, rows, :], cols)
        if diagonal:
            i = lax.broadcasted_iota(jnp.int32, squared.shape, 0) + start
            j = lax.broadcasted_iota(jnp.int32, squared.shape, 1)
            squared = jnp.where(i == j, 0.0, squared)
            projected = jnp.where(i == j, 0.0, projected)
            inverse = lax.rsqrt(jnp.maximum(squared, 0.25 * SCALE * SCALE))
        else:
            inverse = lax.rsqrt(squared)
        capped = jnp.minimum(inverse, 1.0 / TOUCH)
        capped_sq = capped * capped
        scalar = capped * (2.0 + capped_sq) + jnp.maximum(TOUCH - squared * inverse, 0.0)
        tensor = (capped_sq * (2.0 / 3.0 - capped_sq)) * (inverse * projected)
        s_high, s_low = split2(scalar)
        t_high, t_low = split2(tensor)
        acc_f[rows, :] += dot_nt(s_high, cols) + dot_nt(s_low, cols)
        acc_g[rows, :] += dot_nt(t_high, cols) + dot_nt(t_low, cols)


def delta_of(k, n):
    return (k % 2) * ((k + 1) // 2) + (1 - k % 2) * (n - k // 2)


def kernel(
    n, p_ref, f_ref, it_ref, o_it, o_res, o_dir,
    gath, own_ref, acc_f, acc_g, stat, send_sem, recv_sem, stat_send, stat_recv,
):
    me = lax.axis_index("tile")
    barrier = pltpu.get_barrier_semaphore()

    def peer(k):
        return {"tile": lax.rem(me + delta_of(k, n), n)}

    def source(k):
        return lax.rem(me + n - delta_of(k, n), n)

    @pl.loop(1, n)
    def _(k):
        pl.semaphore_signal(barrier, inc=1, device_id=peer(k), device_id_type=MESH)

    pos = (p_ref[...] - CENTRE) * SCALE
    force = f_ref[...]
    gath[me, 0:3, :] = pos
    gath[me, 3:4, :] = jnp.sum(pos * pos, axis=0, keepdims=True)
    gath[me, 4:7, :] = force
    gath[me, 7:8, :] = jnp.sum(pos * force, axis=0, keepdims=True)

    x = gath[me]
    own_cols = features(x)
    own_t = own_features(x)
    own_ref[0, :, :] = own_t[:, :KDIM].astype(jnp.bfloat16)
    own_ref[1, :, :] = own_t[:, KDIM:].astype(jnp.bfloat16)
    acc_f[...] = jnp.zeros_like(acc_f)
    acc_g[...] = jnp.zeros_like(acc_g)

    pl.semaphore_wait(barrier, n - 1)

    def block_copy(k):
        return pltpu.make_async_remote_copy(
            src_ref=gath.at[me], dst_ref=gath.at[me], send_sem=send_sem.at[k], recv_sem=recv_sem.at[k],
            device_id=peer(k), device_id_type=MESH,
        )

    def block_arrival(k):
        return pltpu.make_async_remote_copy(
            src_ref=gath.at[source(k)], dst_ref=gath.at[source(k)], send_sem=send_sem.at[k], recv_sem=recv_sem.at[k],
            device_id=peer(k), device_id_type=MESH,
        )

    @pl.loop(1, n)
    def _(k):
        block_copy(k).start()

    pair_block(own_cols, own_ref, acc_f, acc_g, True)

    @pl.loop(1, n)
    def _(k):
        block_arrival(k).wait_recv()
        pair_block(features(gath[source(k)]), own_ref, acc_f, acc_g, False)

    sum_f = acc_f[...].T
    sum_g = acc_g[...].T
    c_part = sum_f[4:7] + (sum_f[12:15] + sum_f[20:23])
    g_pos = sum_g[0:3] + (sum_g[8:11] + sum_g[16:19])
    g_all = sum_g[48:49]
    image = FACTOR * (c_part + 3.0 * (pos * g_all - g_pos))

    def lanes(v):
        total = jnp.sum(v, axis=0, keepdims=True)
        part = total[:, 0:128]
        for s in range(128, total.shape[1], 128):
            part = part + total[:, s : s + 128]
        return part

    row = lax.broadcasted_iota(jnp.int32, (8, 128), 0)
    stat[me] = jnp.where(
        row == 0, lanes(force * force),
        jnp.where(row == 1, lanes(force * image), jnp.where(row == 2, lanes(image * image), 0.0)),
    )

    def stat_copy(k):
        return pltpu.make_async_remote_copy(
            src_ref=stat.at[me], dst_ref=stat.at[me], send_sem=stat_send.at[k], recv_sem=stat_recv.at[k],
            device_id=peer(k), device_id_type=MESH,
        )

    def stat_arrival(k):
        return pltpu.make_async_remote_copy(
            src_ref=stat.at[source(k)], dst_ref=stat.at[source(k)], send_sem=stat_send.at[k], recv_sem=stat_recv.at[k],
            device_id=peer(k), device_id_type=MESH,
        )

    @pl.loop(1, n)
    def _(k):
        stat_copy(k).start()

    @pl.loop(1, n)
    def _(k):
        block_copy(k).wait_send()

    @pl.loop(1, n)
    def _(k):
        stat_arrival(k).wait_recv()

    total = jnp.sum(stat[...], axis=0)
    total = jnp.sum(total, axis=1, keepdims=True)
    old_norm = total[0:1]
    step = old_norm / total[1:2]
    new_norm = step * step * total[2:3] - old_norm
    new_residual = force - step * image
    o_it[...] = it_ref[...] + step * force
    o_res[...] = new_residual
    o_dir[...] = new_residual + (new_norm / old_norm) * force

    @pl.loop(1, n)
    def _(k):
        stat_copy(k).wait_send()


def solution(mesh):
    n = mesh.shape["tile"]

    def shards(positions, residual, iterate):
        dims, size = positions.shape
        out = jax.ShapeDtypeStruct((dims, size), jnp.float32)
        spec = pl.BlockSpec(memory_space=pltpu.VMEM)
        return pl.pallas_call(
            functools.partial(kernel, n),
            out_shape=(out, out, out),
            in_specs=[spec] * 3,
            out_specs=(spec,) * 3,
            scratch_shapes=[
                pltpu.VMEM((n, 8, size), jnp.float32),
                pltpu.VMEM((2, size, KDIM), jnp.bfloat16),
                pltpu.VMEM((size, KDIM), jnp.float32),
                pltpu.VMEM((size, KDIM), jnp.float32),
                pltpu.VMEM((n, 8, 128), jnp.float32),
                pltpu.SemaphoreType.DMA((n,)),
                pltpu.SemaphoreType.DMA((n,)),
                pltpu.SemaphoreType.DMA((n,)),
                pltpu.SemaphoreType.DMA((n,)),
            ],
            compiler_params=pltpu.CompilerParams(collective_id=0, has_side_effects=True),
        )(positions, residual, iterate)

    spec = P("real", "tile")
    return jax.shard_map(
        shards, mesh=mesh, in_specs=(spec, spec, spec), out_specs=(spec, spec, spec), check_vma=False
    )
```

```python
import functools
import math

import jax
import jax.numpy as jnp
from jax import lax
from jax.experimental import pallas as pl
from jax.experimental.pallas import tpu as pltpu
from jax.sharding import PartitionSpec as P

MESH = pl.DeviceIdType.MESH
CENTRE = 62.0
SCALE = math.sqrt(0.75)
TOUCH = math.sqrt(3.0)
FACTOR = SCALE**3 / 2.0
ROWS = 128
KDIM = 64


def split3(x):
    high = x.astype(jnp.bfloat16).astype(jnp.float32)
    rest = x - high
    mid = rest.astype(jnp.bfloat16).astype(jnp.float32)
    return high, mid, rest - mid


def split2(x):
    high = x.astype(jnp.bfloat16)
    return high, (x - high.astype(jnp.float32)).astype(jnp.bfloat16)


def dot_nn(a, b):
    return lax.dot_general(a, b, (((1,), (0,)), ((), ())), preferred_element_type=jnp.float32)


def dot_nt(a, b):
    return lax.dot_general(a, b, (((1,), (1,)), ((), ())), preferred_element_type=jnp.float32)


def columns(x):
    high, mid, low = split3(x)
    row = lax.broadcasted_iota(jnp.int32, x.shape, 0)
    ones = jnp.where(row < 3, 1.0, 0.0).astype(jnp.float32)
    return jnp.concatenate(
        [high, mid, low, high, mid, high, ones, jnp.zeros_like(x)], axis=0
    ).astype(jnp.bfloat16)


def weights(x):
    row = lax.broadcasted_iota(jnp.int32, x.shape, 0)
    doubled = jnp.where(row < 4, pltpu.roll(x, 4, 0), x)
    first = doubled * jnp.where(row < 4, x[0:1], 1.0)
    second = doubled * jnp.where(row < 4, x[1:2], x[2:3])
    zero = jnp.zeros_like(x)
    return jnp.concatenate([*split3(first), *split3(second), zero, zero], axis=0).astype(jnp.bfloat16)


def own_rows(x):
    high, mid, low = split3(x)
    row = lax.broadcasted_iota(jnp.int32, x.shape, 0)
    zero = jnp.zeros_like(x)
    h, m, l = [jnp.where(row < 3, -2.0 * part, zero) for part in (high, mid, low)]
    h = jnp.where(row == 3, 1.0, h)
    own = jnp.where(row == 0, high[3:4], jnp.where(row == 1, mid[3:4], jnp.where(row == 2, low[3:4], zero)))
    return jnp.concatenate([h, h, h, m, m, l, own, zero] + [zero] * 8, axis=0).T


def combine(sum_f, sum_h, pos):
    scalar = sum_f[4:7] + (sum_f[12:15] + sum_f[20:23])
    first = sum_h[0:8] + (sum_h[8:16] + sum_h[16:24])
    second = sum_h[24:32] + (sum_h[32:40] + sum_h[40:48])
    along = jnp.sum(pos * first[4:7], axis=0, keepdims=True) - first[7:8]
    mixed = jnp.concatenate(
        [
            part[3:4] - jnp.sum(pos * part[0:3], axis=0, keepdims=True)
            for part in (first[0:4], second[0:4], second[4:8])
        ],
        axis=0,
    )
    return scalar + 3.0 * (pos * along + mixed)


def pair_block(x, own_ref, own_weights, acc_f, acc_h, far_f, far_h, diagonal):
    size = own_ref.shape[0]
    cols = columns(x)
    wide = weights(x)
    twice = jnp.concatenate([wide, wide], axis=1)
    for start in range(0, size, ROWS):
        rows = slice(start, start + ROWS)
        squared = dot_nn(own_ref[rows, :], cols)
        if diagonal:
            i = lax.broadcasted_iota(jnp.int32, squared.shape, 0) + start
            j = lax.broadcasted_iota(jnp.int32, squared.shape, 1)
            squared = jnp.where(i == j, 0.0, squared)
            inverse = lax.rsqrt(jnp.maximum(squared, 0.25 * SCALE * SCALE))
        else:
            inverse = lax.rsqrt(squared)
        capped = jnp.minimum(inverse, 1.0 / TOUCH)
        capped_sq = capped * capped
        scalar = capped * (2.0 + capped_sq) + jnp.maximum(TOUCH - squared * inverse, 0.0)
        tensor = (capped_sq * (2.0 / 3.0 - capped_sq)) * inverse
        if diagonal:
            tensor = jnp.where(i == j, 0.0, tensor)
        s_high, s_low = split2(scalar)
        t_high, t_low = split2(tensor)
        acc_f[rows, :] += dot_nt(jnp.concatenate([s_high, s_low], axis=1), twice)
        acc_h[rows, :] += dot_nt(jnp.concatenate([t_high, t_low], axis=1), twice)
        if far_f is not None:
            own = own_weights[:, rows]
            own = jnp.concatenate([own, own], axis=1)
            out_f = dot_nn(own, jnp.concatenate([s_high, s_low], axis=0))
            out_h = dot_nn(own, jnp.concatenate([t_high, t_low], axis=0))
            if start == 0:
                far_f[...] = out_f
                far_h[...] = out_h
            else:
                far_f[...] += out_f
                far_h[...] += out_h


def kernel(
    n, p_ref, f_ref, it_ref, o_it, o_res, o_dir,
    gath, own_ref, own_w, acc_f, acc_h, far_f, far_h, give, take, stat,
    send_sem, recv_sem, give_sem, take_sem, stat_send, stat_recv,
):
    me = lax.axis_index("tile")
    half = n // 2
    barrier = pltpu.get_barrier_semaphore()

    def ahead(k):
        return lax.rem(me + k, n)

    def behind(k):
        return lax.rem(me + n - k, n)

    @pl.loop(1, n)
    def _(k):
        pl.semaphore_signal(barrier, inc=1, device_id={"tile": ahead(k)}, device_id_type=MESH)

    pos = (p_ref[...] - CENTRE) * SCALE
    force = f_ref[...]
    gath[me, 0:3, :] = pos
    gath[me, 3:4, :] = jnp.sum(pos * pos, axis=0, keepdims=True)
    gath[me, 4:7, :] = force
    gath[me, 7:8, :] = jnp.sum(pos * force, axis=0, keepdims=True)

    x = gath[me]
    own_ref[...] = own_rows(x)[:, :KDIM].astype(jnp.bfloat16)
    own_w[...] = weights(x)
    acc_f[...] = jnp.zeros_like(acc_f)
    acc_h[...] = jnp.zeros_like(acc_h)

    pl.semaphore_wait(barrier, n - 1)

    def block_copy(k, slot):
        return pltpu.make_async_remote_copy(
            src_ref=gath.at[slot], dst_ref=gath.at[slot], send_sem=send_sem.at[k], recv_sem=recv_sem.at[k],
            device_id={"tile": behind(k)}, device_id_type=MESH,
        )

    def give_copy(k):
        return pltpu.make_async_remote_copy(
            src_ref=give.at[k], dst_ref=take.at[k], send_sem=give_sem.at[k], recv_sem=take_sem.at[k],
            device_id={"tile": ahead(k)}, device_id_type=MESH,
        )

    def stat_copy(k, slot):
        return pltpu.make_async_remote_copy(
            src_ref=stat.at[slot], dst_ref=stat.at[slot], send_sem=stat_send.at[k], recv_sem=stat_recv.at[k],
            device_id={"tile": ahead(k)}, device_id_type=MESH,
        )

    @pl.loop(1, half + 1)
    def _(k):
        block_copy(k, me).start()

    pair_block(x, own_ref, own_w, acc_f, acc_h, None, None, True)

    @pl.loop(1, half)
    def _(k):
        block_copy(k, ahead(k)).wait_recv()

        @pl.when(k > 1)
        def _():
            give_copy(k - 1).start()

        other = gath[ahead(k)]
        pair_block(other, own_ref, own_w, acc_f, acc_h, far_f, far_h, False)
        give[k, 0:3, :] = combine(far_f[...], far_h[...], other[0:3])

    block_copy(half, ahead(half)).wait_recv()
    if half > 1:
        give_copy(half - 1).start()
    pair_block(gath[ahead(half)], own_ref, own_w, acc_f, acc_h, None, None, False)

    image = combine(acc_f[...].T, acc_h[...].T, pos)

    def added(k, running):
        give_copy(k).wait_recv()
        return running + take[k, 0:3, :]

    image = FACTOR * lax.fori_loop(1, half, added, image)

    def lanes(v):
        total = jnp.sum(v, axis=0, keepdims=True)
        part = total[:, 0:128]
        for s in range(128, total.shape[1], 128):
            part = part + total[:, s : s + 128]
        return part

    row = lax.broadcasted_iota(jnp.int32, (8, 128), 0)
    stat[me] = jnp.where(
        row == 0, lanes(force * force),
        jnp.where(row == 1, lanes(force * image), jnp.where(row == 2, lanes(image * image), 0.0)),
    )

    @pl.loop(1, n)
    def _(k):
        stat_copy(k, me).start()

    @pl.loop(1, half + 1)
    def _(k):
        block_copy(k, me).wait_send()

    @pl.loop(1, half)
    def _(k):
        give_copy(k).wait_send()

    @pl.loop(1, n)
    def _(k):
        stat_copy(k, behind(k)).wait_recv()

    total = jnp.sum(stat[...], axis=0)
    total = jnp.sum(total, axis=1, keepdims=True)
    old_norm = total[0:1]
    step = old_norm / total[1:2]
    new_norm = step * step * total[2:3] - old_norm
    new_residual = force - step * image
    o_it[...] = it_ref[...] + step * force
    o_res[...] = new_residual
    o_dir[...] = new_residual + (new_norm / old_norm) * force

    @pl.loop(1, n)
    def _(k):
        stat_copy(k, me).wait_send()


def solution(mesh):
    n = mesh.shape["tile"]

    def shards(positions, residual, iterate):
        dims, size = positions.shape
        out = jax.ShapeDtypeStruct((dims, size), jnp.float32)
        spec = pl.BlockSpec(memory_space=pltpu.VMEM)
        return pl.pallas_call(
            functools.partial(kernel, n),
            out_shape=(out, out, out),
            in_specs=[spec] * 3,
            out_specs=(spec,) * 3,
            scratch_shapes=[
                pltpu.VMEM((n, 8, size), jnp.float32),
                pltpu.VMEM((size, KDIM), jnp.bfloat16),
                pltpu.VMEM((KDIM, size), jnp.bfloat16),
                pltpu.VMEM((size, KDIM), jnp.float32),
                pltpu.VMEM((size, KDIM), jnp.float32),
                pltpu.VMEM((KDIM, size), jnp.float32),
                pltpu.VMEM((KDIM, size), jnp.float32),
                pltpu.VMEM((n // 2, 8, size), jnp.float32),
                pltpu.VMEM((n // 2, 8, size), jnp.float32),
                pltpu.VMEM((n, 8, 128), jnp.float32),
                pltpu.SemaphoreType.DMA((n // 2 + 1,)),
                pltpu.SemaphoreType.DMA((n // 2 + 1,)),
                pltpu.SemaphoreType.DMA((n // 2,)),
                pltpu.SemaphoreType.DMA((n // 2,)),
                pltpu.SemaphoreType.DMA((n,)),
                pltpu.SemaphoreType.DMA((n,)),
            ],
            compiler_params=pltpu.CompilerParams(collective_id=0, has_side_effects=True),
        )(positions, residual, iterate)

    spec = P("real", "tile")
    return jax.shard_map(
        shards, mesh=mesh, in_specs=(spec, spec, spec), out_specs=(spec, spec, spec), check_vma=False
    )
```

```python
import functools
import math

import jax
import jax.numpy as jnp
from jax import lax
from jax.experimental import pallas as pl
from jax.experimental.pallas import tpu as pltpu
from jax.sharding import PartitionSpec as P

MESH = pl.DeviceIdType.MESH
CENTRE = 62.0
SCALE = math.sqrt(0.75)
TOUCH = math.sqrt(3.0)
FACTOR = SCALE**3 / 2.0
ROWS = 512
AHEAD = 2
KDIM = 64


def split3(x):
    high = x.astype(jnp.bfloat16).astype(jnp.float32)
    rest = x - high
    mid = rest.astype(jnp.bfloat16).astype(jnp.float32)
    return high, mid, rest - mid


def split2(x):
    high = x.astype(jnp.bfloat16)
    return high, (x - high.astype(jnp.float32)).astype(jnp.bfloat16)


def dot_nn(a, b):
    return lax.dot_general(a, b, (((1,), (0,)), ((), ())), preferred_element_type=jnp.float32)


def dot_nt(a, b):
    return lax.dot_general(a, b, (((1,), (1,)), ((), ())), preferred_element_type=jnp.float32)


def columns(x):
    high, mid, low = split3(x)
    row = lax.broadcasted_iota(jnp.int32, x.shape, 0)
    ones = jnp.where(row < 3, 1.0, 0.0).astype(jnp.float32)
    return jnp.concatenate(
        [high, mid, low, high, mid, high, ones, jnp.zeros_like(x)], axis=0
    ).astype(jnp.bfloat16)


def weights(x):
    row = lax.broadcasted_iota(jnp.int32, x.shape, 0)
    doubled = jnp.where(row < 4, pltpu.roll(x, 4, 0), x)
    first = doubled * jnp.where(row < 4, x[0:1], 1.0)
    second = doubled * jnp.where(row < 4, x[1:2], x[2:3])
    zero = jnp.zeros_like(x)
    return jnp.concatenate([*split3(first), *split3(second), zero, zero], axis=0).astype(jnp.bfloat16)


def own_rows(x):
    high, mid, low = split3(x)
    row = lax.broadcasted_iota(jnp.int32, x.shape, 0)
    zero = jnp.zeros_like(x)
    h, m, l = [jnp.where(row < 3, -2.0 * part, zero) for part in (high, mid, low)]
    h = jnp.where(row == 3, 1.0, h)
    own = jnp.where(row == 0, high[3:4], jnp.where(row == 1, mid[3:4], jnp.where(row == 2, low[3:4], zero)))
    return jnp.concatenate([h, h, h, m, m, l, own, zero] + [zero] * 8, axis=0).T


def combine(sum_f, sum_h, pos):
    scalar = sum_f[4:7] + (sum_f[12:15] + sum_f[20:23])
    first = sum_h[0:8] + (sum_h[8:16] + sum_h[16:24])
    second = sum_h[24:32] + (sum_h[32:40] + sum_h[40:48])
    along = jnp.sum(pos * first[4:7], axis=0, keepdims=True) - first[7:8]
    mixed = jnp.concatenate(
        [
            part[3:4] - jnp.sum(pos * part[0:3], axis=0, keepdims=True)
            for part in (first[0:4], second[0:4], second[4:8])
        ],
        axis=0,
    )
    return scalar + 3.0 * (pos * along + mixed)


def pair_block(x, own_ref, own_weights, acc_f, acc_h, far_f, far_h, diagonal):
    size = own_ref.shape[0]
    cols = columns(x)
    wide = weights(x)
    twice = jnp.concatenate([wide, wide], axis=1)
    for start in range(0, size, ROWS):
        rows = slice(start, start + ROWS)
        squared = dot_nn(own_ref[rows, :], cols)
        if diagonal:
            i = lax.broadcasted_iota(jnp.int32, squared.shape, 0) + start
            j = lax.broadcasted_iota(jnp.int32, squared.shape, 1)
            squared = jnp.where(i == j, 0.0, squared)
            inverse = lax.rsqrt(jnp.maximum(squared, 0.25 * SCALE * SCALE))
        else:
            inverse = lax.rsqrt(squared)
        capped = jnp.minimum(inverse, 1.0 / TOUCH)
        capped_sq = capped * capped
        scalar = capped * (2.0 + capped_sq) + jnp.maximum(TOUCH - squared * inverse, 0.0)
        tensor = (capped_sq * (2.0 / 3.0 - capped_sq)) * inverse
        if diagonal:
            tensor = jnp.where(i == j, 0.0, tensor)
        s_high, s_low = split2(scalar)
        t_high, t_low = split2(tensor)
        acc_f[rows, :] += dot_nt(jnp.concatenate([s_high, s_low], axis=1), twice)
        acc_h[rows, :] += dot_nt(jnp.concatenate([t_high, t_low], axis=1), twice)
        if far_f is not None:
            own = own_weights[:, rows]
            own = jnp.concatenate([own, own], axis=1)
            out_f = dot_nn(own, jnp.concatenate([s_high, s_low], axis=0))
            out_h = dot_nn(own, jnp.concatenate([t_high, t_low], axis=0))
            if start == 0:
                far_f[...] = out_f
                far_h[...] = out_h
            else:
                far_f[...] += out_f
                far_h[...] += out_h


def kernel(
    n, p_ref, f_ref, o_image, o_step, o_ratio,
    gath, own_ref, own_w, acc_f, acc_h, far_f, far_h, give, take, stat,
    send_sem, recv_sem, give_sem, take_sem, stat_send, stat_recv,
):
    me = lax.axis_index("tile")
    half = n // 2
    barrier = pltpu.get_barrier_semaphore()

    def ahead(k):
        return lax.rem(me + k, n)

    def behind(k):
        return lax.rem(me + n - k, n)

    @pl.loop(1, n)
    def _(k):
        pl.semaphore_signal(barrier, inc=1, device_id={"tile": ahead(k)}, device_id_type=MESH)

    pos = (p_ref[...] - CENTRE) * SCALE
    force = f_ref[...]
    gath[me, 0:3, :] = pos
    gath[me, 3:4, :] = jnp.sum(pos * pos, axis=0, keepdims=True)
    gath[me, 4:7, :] = force
    gath[me, 7:8, :] = jnp.sum(pos * force, axis=0, keepdims=True)

    x = gath[me]
    own_ref[...] = own_rows(x)[:, :KDIM].astype(jnp.bfloat16)
    own_w[...] = weights(x)
    acc_f[...] = jnp.zeros_like(acc_f)
    acc_h[...] = jnp.zeros_like(acc_h)

    pl.semaphore_wait(barrier, n - 1)

    def block_copy(k, slot):
        return pltpu.make_async_remote_copy(
            src_ref=gath.at[slot], dst_ref=gath.at[slot], send_sem=send_sem.at[k], recv_sem=recv_sem.at[k],
            device_id={"tile": behind(k)}, device_id_type=MESH,
        )

    def give_copy(k):
        return pltpu.make_async_remote_copy(
            src_ref=give.at[k], dst_ref=take.at[k], send_sem=give_sem.at[k], recv_sem=take_sem.at[k],
            device_id={"tile": ahead(k)}, device_id_type=MESH,
        )

    def stat_copy(k, slot):
        return pltpu.make_async_remote_copy(
            src_ref=stat.at[slot], dst_ref=stat.at[slot], send_sem=stat_send.at[k], recv_sem=stat_recv.at[k],
            device_id={"tile": ahead(k)}, device_id_type=MESH,
        )

    @pl.loop(1, min(AHEAD, half) + 1)
    def _(k):
        block_copy(k, me).start()

    pair_block(x, own_ref, own_w, acc_f, acc_h, None, None, True)

    @pl.loop(1, half)
    def _(k):
        @pl.when(k + AHEAD <= half)
        def _():
            block_copy(k + AHEAD, me).start()

        block_copy(k, ahead(k)).wait_recv()

        @pl.when(k > 1)
        def _():
            give_copy(k - 1).start()

        other = gath[ahead(k)]
        pair_block(other, own_ref, own_w, acc_f, acc_h, far_f, far_h, False)
        give[k] = combine(far_f[...], far_h[...], other[0:3])

    block_copy(half, ahead(half)).wait_recv()
    if half > 1:
        give_copy(half - 1).start()
    pair_block(gath[ahead(half)], own_ref, own_w, acc_f, acc_h, None, None, False)

    image = combine(acc_f[...].T, acc_h[...].T, pos)

    def added(k, running):
        give_copy(k).wait_recv()
        return running + take[k]

    image = FACTOR * lax.fori_loop(1, half, added, image)

    def whole(v):
        return jnp.sum(jnp.sum(v, axis=0, keepdims=True), axis=1, keepdims=True)

    lane = lax.broadcasted_iota(jnp.int32, (1, 128), 1)
    stat[me] = jnp.where(
        lane == 0, whole(force * force),
        jnp.where(lane == 1, whole(force * image), jnp.where(lane == 2, whole(image * image), 0.0)),
    )

    @pl.loop(1, n)
    def _(k):
        stat_copy(k, me).start()

    @pl.loop(1, half + 1)
    def _(k):
        block_copy(k, me).wait_send()

    @pl.loop(1, half)
    def _(k):
        give_copy(k).wait_send()

    @pl.loop(1, n)
    def _(k):
        stat_copy(k, behind(k)).wait_recv()

    total = jnp.sum(stat[...], axis=0)
    old_norm = total[:, 0:1]
    step = old_norm / total[:, 1:2]
    new_norm = step * step * total[:, 2:3] - old_norm
    o_image[...] = image
    o_step[...] = jnp.broadcast_to(step, image.shape)
    o_ratio[...] = jnp.broadcast_to(new_norm / old_norm, image.shape)

    @pl.loop(1, n)
    def _(k):
        stat_copy(k, me).wait_send()


def solution(mesh):
    n = mesh.shape["tile"]

    def shards(positions, residual, iterate):
        dims, size = positions.shape
        out = jax.ShapeDtypeStruct((dims, size), jnp.float32)
        spec = pl.BlockSpec(memory_space=pltpu.VMEM)
        image, step, ratio = pl.pallas_call(
            functools.partial(kernel, n),
            out_shape=(out, out, out),
            in_specs=[spec] * 2,
            out_specs=(spec,) * 3,
            scratch_shapes=[
                pltpu.VMEM((n, 8, size), jnp.float32),
                pltpu.VMEM((size, KDIM), jnp.bfloat16),
                pltpu.VMEM((KDIM, size), jnp.bfloat16),
                pltpu.VMEM((size, KDIM), jnp.float32),
                pltpu.VMEM((size, KDIM), jnp.float32),
                pltpu.VMEM((KDIM, size), jnp.float32),
                pltpu.VMEM((KDIM, size), jnp.float32),
                pltpu.VMEM((n // 2, 3, size), jnp.float32),
                pltpu.VMEM((n // 2, 3, size), jnp.float32),
                pltpu.VMEM((n, 1, 128), jnp.float32),
                pltpu.SemaphoreType.DMA((n // 2 + 1,)),
                pltpu.SemaphoreType.DMA((n // 2 + 1,)),
                pltpu.SemaphoreType.DMA((n // 2,)),
                pltpu.SemaphoreType.DMA((n // 2,)),
                pltpu.SemaphoreType.DMA((n,)),
                pltpu.SemaphoreType.DMA((n,)),
            ],
            compiler_params=pltpu.CompilerParams(collective_id=0, has_side_effects=True),
        )(positions, residual)
        new_residual = residual - step * image
        return iterate + step * residual, new_residual, new_residual + ratio * residual

    spec = P("real", "tile")
    return jax.shard_map(
        shards, mesh=mesh, in_specs=(spec, spec, spec), out_specs=(spec, spec, spec), check_vma=False
    )
```

```python
import functools
import math

import jax
import jax.numpy as jnp
from jax import lax
from jax.experimental import pallas as pl
from jax.experimental.pallas import tpu as pltpu
from jax.sharding import PartitionSpec as P

MESH = pl.DeviceIdType.MESH
CENTRE = 62.0
SCALE = math.sqrt(0.75)
TOUCH = math.sqrt(3.0)
FACTOR = SCALE**3 / 2.0
ROWS = 512
AHEAD = 2
KDIM = 64
WDIM = 48


def split3(x):
    high = x.astype(jnp.bfloat16).astype(jnp.float32)
    rest = x - high
    mid = rest.astype(jnp.bfloat16).astype(jnp.float32)
    return high, mid, rest - mid


def split2(x):
    high = x.astype(jnp.bfloat16)
    return high, (x - high.astype(jnp.float32)).astype(jnp.bfloat16)


def dot_nn(a, b):
    return lax.dot_general(a, b, (((1,), (0,)), ((), ())), preferred_element_type=jnp.float32)


def dot_nt(a, b):
    return lax.dot_general(a, b, (((1,), (1,)), ((), ())), preferred_element_type=jnp.float32)


def columns(x):
    high, mid, low = split3(x)
    row = lax.broadcasted_iota(jnp.int32, x.shape, 0)
    ones = jnp.where(row < 3, 1.0, 0.0).astype(jnp.float32)
    return jnp.concatenate(
        [high, mid, low, high, mid, high, ones, jnp.zeros_like(x)], axis=0
    ).astype(jnp.bfloat16)


def weights(x):
    row = lax.broadcasted_iota(jnp.int32, x.shape, 0)
    doubled = jnp.where(row < 4, pltpu.roll(x, 4, 0), x)
    first = doubled * jnp.where(row < 4, x[0:1], 1.0)
    second = doubled * jnp.where(row < 4, x[1:2], x[2:3])
    return jnp.concatenate([*split3(first), *split3(second)], axis=0).astype(jnp.bfloat16)


def own_rows(x):
    high, mid, low = split3(x)
    row = lax.broadcasted_iota(jnp.int32, x.shape, 0)
    zero = jnp.zeros_like(x)
    h, m, l = [jnp.where(row < 3, -2.0 * part, zero) for part in (high, mid, low)]
    h = jnp.where(row == 3, 1.0, h)
    own = jnp.where(row == 0, high[3:4], jnp.where(row == 1, mid[3:4], jnp.where(row == 2, low[3:4], zero)))
    return jnp.concatenate([h, h, h, m, m, l, own, zero] + [zero] * 8, axis=0).T


def combine(sum_f, sum_h, pos):
    scalar = sum_f[4:7] + (sum_f[12:15] + sum_f[20:23])
    first = sum_h[0:8] + (sum_h[8:16] + sum_h[16:24])
    second = sum_h[24:32] + (sum_h[32:40] + sum_h[40:48])
    along = jnp.sum(pos * first[4:7], axis=0, keepdims=True) - first[7:8]
    mixed = jnp.concatenate(
        [
            part[3:4] - jnp.sum(pos * part[0:3], axis=0, keepdims=True)
            for part in (first[0:4], second[0:4], second[4:8])
        ],
        axis=0,
    )
    return scalar + 3.0 * (pos * along + mixed)


def pair_block(x, own_ref, own_weights, acc_f, acc_h, far_f, far_h, diagonal):
    size = own_ref.shape[0]
    cols = columns(x)
    wide = weights(x)
    twice = jnp.concatenate([wide, wide], axis=1)
    for start in range(0, size, ROWS):
        rows = slice(start, start + ROWS)
        squared = dot_nn(own_ref[rows, :], cols)
        if diagonal:
            i = lax.broadcasted_iota(jnp.int32, squared.shape, 0) + start
            j = lax.broadcasted_iota(jnp.int32, squared.shape, 1)
            squared = jnp.where(i == j, 0.0, squared)
            inverse = lax.rsqrt(jnp.maximum(squared, 0.25 * SCALE * SCALE))
        else:
            inverse = lax.rsqrt(squared)
        capped = jnp.minimum(inverse, 1.0 / TOUCH)
        capped_sq = capped * capped
        scalar = capped * (2.0 + capped_sq) + jnp.maximum(TOUCH - squared * inverse, 0.0)
        tensor = (capped_sq * (2.0 / 3.0 - capped_sq)) * inverse
        if diagonal:
            tensor = jnp.where(i == j, 0.0, tensor)
        s_high, s_low = split2(scalar)
        t_high, t_low = split2(tensor)
        acc_f[:, rows] += dot_nt(twice, jnp.concatenate([s_high, s_low], axis=1))
        acc_h[:, rows] += dot_nt(twice, jnp.concatenate([t_high, t_low], axis=1))
        if far_f is not None:
            own = own_weights[:, rows]
            own = jnp.concatenate([own, own], axis=1)
            out_f = dot_nn(own, jnp.concatenate([s_high, s_low], axis=0))
            out_h = dot_nn(own, jnp.concatenate([t_high, t_low], axis=0))
            if start == 0:
                far_f[...] = out_f
                far_h[...] = out_h
            else:
                far_f[...] += out_f
                far_h[...] += out_h


def kernel(
    n, p_ref, f_ref, o_image, o_step, o_ratio,
    gath, own_ref, own_w, acc_f, acc_h, far_f, far_h, give, take, stat,
    send_sem, recv_sem, give_sem, take_sem, stat_send, stat_recv,
):
    me = lax.axis_index("tile")
    half = n // 2
    barrier = pltpu.get_barrier_semaphore()

    def ahead(k):
        return lax.rem(me + k, n)

    def behind(k):
        return lax.rem(me + n - k, n)

    @pl.loop(1, n, unroll=n <= 16)
    def _(k):
        pl.semaphore_signal(barrier, inc=1, device_id={"tile": ahead(k)}, device_id_type=MESH)

    pos = (p_ref[...] - CENTRE) * SCALE
    force = f_ref[...]
    gath[me, 0:3, :] = pos
    gath[me, 3:4, :] = jnp.sum(pos * pos, axis=0, keepdims=True)
    gath[me, 4:7, :] = force
    gath[me, 7:8, :] = jnp.sum(pos * force, axis=0, keepdims=True)

    x = gath[me]
    own_ref[...] = own_rows(x)[:, :KDIM].astype(jnp.bfloat16)
    own_w[...] = weights(x)
    acc_f[...] = jnp.zeros_like(acc_f)
    acc_h[...] = jnp.zeros_like(acc_h)

    pair_block(x, own_ref, own_w, acc_f, acc_h, None, None, True)
    pl.semaphore_wait(barrier, n - 1)

    def block_copy(k, slot):
        return pltpu.make_async_remote_copy(
            src_ref=gath.at[slot], dst_ref=gath.at[slot], send_sem=send_sem.at[k], recv_sem=recv_sem.at[k],
            device_id={"tile": behind(k)}, device_id_type=MESH,
        )

    def give_copy(k):
        return pltpu.make_async_remote_copy(
            src_ref=give.at[k], dst_ref=take.at[k], send_sem=give_sem.at[k], recv_sem=take_sem.at[k],
            device_id={"tile": ahead(k)}, device_id_type=MESH,
        )

    def stat_copy(k, slot):
        return pltpu.make_async_remote_copy(
            src_ref=stat.at[slot], dst_ref=stat.at[slot], send_sem=stat_send.at[k], recv_sem=stat_recv.at[k],
            device_id={"tile": ahead(k)}, device_id_type=MESH,
        )

    @pl.loop(1, min(AHEAD, half) + 1)
    def _(k):
        block_copy(k, me).start()

    @pl.loop(1, half)
    def _(k):
        @pl.when(k + AHEAD <= half)
        def _():
            block_copy(k + AHEAD, me).start()

        block_copy(k, ahead(k)).wait_recv()

        @pl.when(k > 1)
        def _():
            give_copy(k - 1).start()

        other = gath[ahead(k)]
        pair_block(other, own_ref, own_w, acc_f, acc_h, far_f, far_h, False)
        give[k] = combine(far_f[...], far_h[...], other[0:3])

    block_copy(half, ahead(half)).wait_recv()
    if half > 1:
        give_copy(half - 1).start()
    pair_block(gath[ahead(half)], own_ref, own_w, acc_f, acc_h, None, None, False)

    image = combine(acc_f[...], acc_h[...], pos)

    def added(k, running):
        give_copy(k).wait_recv()
        return running + take[k]

    image = FACTOR * lax.fori_loop(1, half, added, image)

    def whole(v):
        return jnp.sum(jnp.sum(v, axis=0, keepdims=True), axis=1, keepdims=True)

    lane = lax.broadcasted_iota(jnp.int32, (1, 128), 1)
    stat[me] = jnp.where(
        lane == 0, whole(force * force),
        jnp.where(lane == 1, whole(force * image), jnp.where(lane == 2, whole(image * image), 0.0)),
    )

    @pl.loop(1, n, unroll=n <= 16)
    def _(k):
        stat_copy(k, me).start()

    @pl.loop(1, half + 1)
    def _(k):
        block_copy(k, me).wait_send()

    @pl.loop(1, half)
    def _(k):
        give_copy(k).wait_send()

    @pl.loop(1, n, unroll=n <= 16)
    def _(k):
        stat_copy(k, behind(k)).wait_recv()

    total = jnp.sum(stat[...], axis=0)
    old_norm = total[:, 0:1]
    step = old_norm / total[:, 1:2]
    new_norm = step * step * total[:, 2:3] - old_norm
    o_image[...] = image
    o_step[...] = jnp.broadcast_to(step, image.shape)
    o_ratio[...] = jnp.broadcast_to(new_norm / old_norm, image.shape)

    @pl.loop(1, n, unroll=n <= 16)
    def _(k):
        stat_copy(k, me).wait_send()


def solution(mesh):
    n = mesh.shape["tile"]

    def shards(positions, residual, iterate):
        dims, size = positions.shape
        out = jax.ShapeDtypeStruct((dims, size), jnp.float32)
        spec = pl.BlockSpec(memory_space=pltpu.VMEM)
        image, step, ratio = pl.pallas_call(
            functools.partial(kernel, n),
            out_shape=(out, out, out),
            in_specs=[spec] * 2,
            out_specs=(spec,) * 3,
            scratch_shapes=[
                pltpu.VMEM((n, 8, size), jnp.float32),
                pltpu.VMEM((size, KDIM), jnp.bfloat16),
                pltpu.VMEM((WDIM, size), jnp.bfloat16),
                pltpu.VMEM((WDIM, size), jnp.float32),
                pltpu.VMEM((WDIM, size), jnp.float32),
                pltpu.VMEM((WDIM, size), jnp.float32),
                pltpu.VMEM((WDIM, size), jnp.float32),
                pltpu.VMEM((n // 2, 3, size), jnp.float32),
                pltpu.VMEM((n // 2, 3, size), jnp.float32),
                pltpu.VMEM((n, 1, 128), jnp.float32),
                pltpu.SemaphoreType.DMA((n // 2 + 1,)),
                pltpu.SemaphoreType.DMA((n // 2 + 1,)),
                pltpu.SemaphoreType.DMA((n // 2,)),
                pltpu.SemaphoreType.DMA((n // 2,)),
                pltpu.SemaphoreType.DMA((n,)),
                pltpu.SemaphoreType.DMA((n,)),
            ],
            compiler_params=pltpu.CompilerParams(collective_id=0, has_side_effects=True),
        )(positions, residual)
        new_residual = residual - step * image
        return iterate + step * residual, new_residual, new_residual + ratio * residual

    spec = P("real", "tile")
    return jax.shard_map(
        shards, mesh=mesh, in_specs=(spec, spec, spec), out_specs=(spec, spec, spec), check_vma=False
    )
```
